1024 devices in a mesh: wide: 64 (over y, z_hi, x), narrow: 16 (over z_lo, core).
Axes of the slice: x: 4, y: 8, z: 16 (z_hi: 2, z_lo: 8; z = z_hi * 8 + z_lo), core: 2. Of those that a mesh axis runs over, the one named last changes fastest.
Arguments:
- state: float32 [2, 67108864], P(None, ('wide', 'narrow')), may hold values from -6 to 6
- gates: float32 [6, 2, 256, 256], replicated
- gate_bits: int32 [6, 8], replicated, may hold values from 7 to 15, as said below
- slot_plan: int32 [10], replicated, may hold values from 7 to 15, as said below
Outputs:
- final_state: float32 [2, 67108864], P(None, ('wide', 'narrow'))
The draws below stay inside these ranges and needn't reach their ends.
Inputs may be any that keep to these rules, and one draw needn't show every extreme that they name: `gate_bits`: each gate's row names 8 different positions. `slot_plan`: the first 4 entries differ from one another, and so do the last 6.
All inputs are finite; a program needn't handle non-finite values.
Results may differ from the reference program's by a relative error of at most 0.0001.
Values sent between devices are 32-bit elements; how exact they have to be, the bound alone decides.
No kernel may reach another device: no remote copies, remote signals or barrier semaphores. Data moves between devices by JAX's collectives and lax.ppermute only.
A program may use at most 32 MiB of HBM per device.

```python
import jax
import jax.numpy as jnp
from jax import lax

GATE_QUBITS = 8
GATE_DIM = 256
GATES = 6
LANE_BITS = 7
LOCAL = 16
NARROW_BITS = 4
WIDE_BITS = 6
TOTAL = 67108864


def draw_gates(key, part):
    keys = jax.random.split(jax.random.fold_in(key, 11), 2)
    real_part = jax.random.normal(keys[0], (GATES, GATE_DIM, GATE_DIM), jnp.float32)
    imag_part = jax.random.normal(keys[1], (GATES, GATE_DIM, GATE_DIM), jnp.float32)
    matrix = lax.complex(real_part, imag_part)
    unitary_q, upper = jnp.linalg.qr(matrix)
    diagonal = jnp.diagonal(upper, axis1=-2, axis2=-1)
    phases = diagonal / jnp.abs(diagonal)
    unitary = unitary_q * phases[:, None, :]
    return jnp.stack([jnp.real(unitary), jnp.imag(unitary)], axis=1).astype(jnp.float32)


def draw_gate_bits(key, part):
    base = jax.random.fold_in(key, 23)
    rows = []
    for index in range(GATES):
        chosen = jax.random.permutation(jax.random.fold_in(base, index), LOCAL - LANE_BITS)[:GATE_QUBITS]
        rows.append((chosen + LANE_BITS).astype(jnp.int32))
    return jnp.stack(rows).astype(jnp.int32)


def draw_slot_plan(key, part):
    base = jax.random.fold_in(key, 37)
    first = jax.random.permutation(jax.random.fold_in(base, 1), LOCAL - LANE_BITS)[:NARROW_BITS]
    second = jax.random.permutation(jax.random.fold_in(base, 2), LOCAL - LANE_BITS)[:WIDE_BITS]
    return (jnp.concatenate([first, second]) + LANE_BITS).astype(jnp.int32)


def block_scale(stream_key, shape, shards, least, top_value):
    gain = 1.0
    for position, blocks in shards:
        draws = jax.random.uniform(jax.random.fold_in(jax.random.fold_in(stream_key, 6), position), (blocks,), jnp.float32, least / len(shards), top_value / len(shards))
        gain = gain * jnp.repeat(jnp.exp(draws), shape[position] // blocks).reshape((-1,) + (1,) * (len(shape) - 1 - position))
    return gain


def scatter_about(key, extent, width, bound, shards=(), kind=jnp.bfloat16):
    values = width * jax.random.normal(key, extent, jnp.float32)
    if shards:
        values = values * block_scale(key, extent, shards, -0.22, 0.18)
    return jnp.clip(values, -bound, bound).astype(kind)


def setup_inputs(seed: int = 0) -> dict:
    splits = jax.random.split(jax.random.key(seed), 5)
    state = scatter_about(splits[0], (2, TOTAL), 1.0, 6.0, ((1, 1024),), jnp.float32)
    gates = draw_gates(jax.random.fold_in(splits[4], 71), 0)
    gate_bits = draw_gate_bits(jax.random.fold_in(splits[4], 71), 0)
    slot_plan = draw_slot_plan(jax.random.fold_in(splits[4], 71), 0)
    return dict(state=state, gates=gates, gate_bits=gate_bits, slot_plan=slot_plan)


def bit_table(weights, nbits):
    low_count = nbits // 2
    high_count = nbits - low_count

    def partial_table(count, offset):
        values = jnp.arange(2 ** count, dtype=jnp.int32)
        places = jnp.arange(count, dtype=jnp.int32)
        bits_of = values[:, None] >> places[None, :] & 1
        return jnp.sum(bits_of * weights[offset:offset + count][None, :], axis=1).astype(jnp.int32)
    return (partial_table(high_count, low_count)[:, None] + partial_table(low_count, 0)[None, :]).reshape(-1).astype(jnp.int32)

def gate_order(qubits, nbits):
    count = qubits.shape[0]
    positions = jnp.arange(nbits, dtype=jnp.int32)
    hits = (positions[:, None] == qubits[None, :]).astype(jnp.int32)
    free_flag = (1 - jnp.sum(hits, axis=1)).astype(jnp.int32)
    ranks = (jnp.cumsum(free_flag) - free_flag).astype(jnp.int32)
    targets = jnp.arange(nbits - count, dtype=jnp.int32)
    picked = (ranks[None, :] == targets[:, None]) & (free_flag[None, :] == 1)
    others = jnp.sum(picked.astype(jnp.int32) * positions[None, :], axis=1).astype(jnp.int32)
    return jnp.concatenate([others, qubits.astype(jnp.int32)]).astype(jnp.int32)

def inverse_weights(order, nbits):
    positions = jnp.arange(nbits, dtype=jnp.int32)
    powers = jnp.left_shift(jnp.int32(1), positions)
    match = (order[None, :] == positions[:, None]).astype(jnp.int32)
    return jnp.sum(match * powers[None, :], axis=1).astype(jnp.int32)

def apply_gate(state, unitary, qubits, nbits):
    order = gate_order(qubits, nbits)
    forward = bit_table(jnp.left_shift(jnp.int32(1), order), nbits)
    moved = state[:, forward]
    dim = unitary.shape[-1]
    moved = moved.reshape(2, dim, -1)
    high = lax.Precision.HIGHEST
    real_part = jnp.dot(unitary[0].astype(jnp.float32), moved[0].astype(jnp.float32), precision=high, preferred_element_type=jnp.float32) - jnp.dot(unitary[1].astype(jnp.float32), moved[1].astype(jnp.float32), precision=high, preferred_element_type=jnp.float32)
    imag_part = jnp.dot(unitary[0].astype(jnp.float32), moved[1].astype(jnp.float32), precision=high, preferred_element_type=jnp.float32) + jnp.dot(unitary[1].astype(jnp.float32), moved[0].astype(jnp.float32), precision=high, preferred_element_type=jnp.float32)
    result = jnp.stack([real_part, imag_part]).reshape(2, -1)
    return result[:, bit_table(inverse_weights(order, nbits), nbits)]

def swap_state(state, nbits, firsts, seconds):
    positions = jnp.arange(nbits, dtype=jnp.int32)
    weights = jnp.left_shift(jnp.int32(1), positions)
    for number in range(len(firsts)):
        upper = jnp.int32(firsts[number])
        lower = seconds[number].astype(jnp.int32)
        weights = jnp.where(positions == upper, jnp.left_shift(jnp.int32(1), lower), jnp.where(positions == lower, jnp.left_shift(jnp.int32(1), upper), weights)).astype(jnp.int32)
    return state[:, bit_table(weights, nbits)]

def reference(state, gates, gate_bits, slot_plan):
    nbits = LOCAL + NARROW_BITS + WIDE_BITS
    third = GATES // 3
    for index in range(third):
        state = apply_gate(state, gates[index], gate_bits[index], nbits)
    state = swap_state(state, nbits, [LOCAL + b for b in range(NARROW_BITS)], [slot_plan[b] for b in range(NARROW_BITS)])
    for index in range(third, 2 * third):
        state = apply_gate(state, gates[index], gate_bits[index], nbits)
    state = swap_state(state, nbits, [LOCAL + NARROW_BITS + b for b in range(WIDE_BITS)], [slot_plan[NARROW_BITS + b] for b in range(WIDE_BITS)])
    for index in range(2 * third, GATES):
        state = apply_gate(state, gates[index], gate_bits[index], nbits)
    return state
```

```python
import functools

import jax
import jax.numpy as jnp
from jax import lax
from jax.experimental import pallas as pl
from jax.experimental.pallas import tpu as pltpu
from jax.sharding import PartitionSpec as P

LANE_BITS = 7
LANES = 2**LANE_BITS
ROW_BITS = 9
ROWS = 2**ROW_BITS
DIM_BITS = 8
DIM = 2**DIM_BITS

BF16 = jnp.bfloat16
F32 = jnp.float32


def mm(a, b):
    return jnp.dot(a, b, preferred_element_type=F32)


def split(x):
    high = x.astype(BF16)
    low = (x - high.astype(F32)).astype(BF16)
    return high, low


def gate_slots(bits, gate):
    used = [bits[gate, j] - LANE_BITS for j in range(DIM_BITS)]
    free = ROW_BITS * (ROW_BITS - 1) // 2 - sum(used)
    return used + [free]


def plan_slots(plan, start, count, rest):
    slots = [plan[start + b] - LANE_BITS for b in range(count)]
    filled = jnp.int32(0)
    for p in range(ROW_BITS):
        rest[filled] = jnp.int32(p)
        taken = functools.reduce(jnp.logical_or, [s == p for s in slots])
        filled = filled + jnp.where(taken, 0, 1).astype(jnp.int32)
    return [rest[k] for k in range(ROW_BITS - count)] + slots


def permutation(source, target, where):
    for place in range(ROW_BITS):
        where[target[place]] = jnp.int32(place)
    lane = lax.broadcasted_iota(jnp.int32, (8, ROWS), 1)
    moved = jnp.zeros((8, ROWS), jnp.int32)
    for place in range(ROW_BITS):
        moved = moved | (((lane >> place) & 1) << where[source[place]])
    row = lax.broadcasted_iota(jnp.int32, (ROWS, ROWS), 0)
    hit = jnp.broadcast_to(moved[:1], (ROWS, ROWS)) == row
    return jnp.where(hit, 1.0, 0.0).astype(BF16)


def stack_gate(real, imag):
    real_high, real_low = split(real)
    imag_high, imag_low = split(imag)
    return jnp.concatenate([real_high, imag_high, real_low, imag_low], axis=0)


def pack_parts(real, imag):
    real_high, real_low = split(real)
    imag_high, imag_low = split(imag)
    return jnp.concatenate([real_high, imag_high, real_low, imag_low], axis=1)


def complex_product(stack, high, low, width):
    half = stack.shape[0] // 2
    quarter = half // 2
    first = mm(stack, high)
    total = first[:half] + first[half:] + mm(stack[:half], low)
    real = total[:quarter, :width] - total[quarter:, width:]
    imag = total[:quarter, width:] + total[quarter:, :width]
    return real, imag


def gate_on_parts(stack, parts, width):
    reals, imags = [], []
    for free in range(2):
        rows = parts[free * DIM : (free + 1) * DIM]
        real, imag = complex_product(stack, rows[:, : 2 * width], rows[:, 2 * width :], width)
        reals.append(real)
        imags.append(imag)
    return jnp.concatenate(reals, axis=0), jnp.concatenate(imags, axis=0)


def first_kernel(narrow_bits, bits, plan, x, gates, out, where, rest):
    natural = list(range(ROW_BITS))
    order_a = gate_slots(bits, 0)
    order_b = gate_slots(bits, 1)
    order_out = plan_slots(plan, 0, narrow_bits, rest)
    parts = pack_parts(x[pl.ds(0, ROWS, stride=2), :], x[pl.ds(1, ROWS, stride=2), :])
    parts = mm(permutation(natural, order_a, where), parts).astype(BF16)
    real, imag = gate_on_parts(stack_gate(gates[0, 0], gates[0, 1]), parts, LANES)
    parts = pack_parts(real, imag)
    parts = mm(permutation(order_a, order_b, where), parts).astype(BF16)
    real, imag = gate_on_parts(stack_gate(gates[1, 0], gates[1, 1]), parts, LANES)
    parts = mm(permutation(order_b, order_out, where), pack_parts(real, imag))
    blocks = out.shape[0]
    shape = (blocks, ROWS // blocks, LANES)
    out[:, 0] = (parts[:, :LANES] + parts[:, 2 * LANES : 3 * LANES]).reshape(shape)
    out[:, 1] = (parts[:, LANES : 2 * LANES] + parts[:, 3 * LANES :]).reshape(shape)


def operator_kernel(section, order_in, order_out, bits, plan, gates, out, where, rest):
    order_a = gate_slots(bits, 2 * section)
    order_b = gate_slots(bits, 2 * section + 1)
    columns = order_in(plan, rest)
    result = order_out(plan, rest)
    pick = permutation(columns, order_a, where)
    stack = stack_gate(gates[0, 0], gates[0, 1])
    picked = [mm(stack, pick[free * DIM : (free + 1) * DIM]).astype(BF16) for free in range(2)]
    parts = jnp.concatenate(
        [
            jnp.concatenate([p[k * DIM : (k + 1) * DIM] for p in picked], axis=0)
            for k in range(4)
        ],
        axis=1,
    )
    parts = mm(permutation(order_a, order_b, where), parts).astype(BF16)
    real, imag = gate_on_parts(stack_gate(gates[1, 0], gates[1, 1]), parts, ROWS)
    final = permutation(order_b, result, where)
    for k, part in enumerate([*split(real), *split(imag)]):
        place = (k % 2) * 2 + k // 2
        out[place * ROWS : (place + 1) * ROWS, :] = mm(final, part).astype(BF16)


def apply_section(stack, x):
    real = x[:, 0].reshape(ROWS, LANES)
    imag = x[:, 1].reshape(ROWS, LANES)
    real_high, real_low = split(real)
    imag_high, imag_low = split(imag)
    high = jnp.concatenate([real_high, imag_high], axis=1)
    low = jnp.concatenate([real_low, imag_low], axis=1)
    return complex_product(stack, high, low, LANES)


def middle_kernel(stack, x, out):
    real, imag = apply_section(stack[...], x[...])
    blocks = out.shape[0]
    shape = (blocks, ROWS // blocks, LANES)
    out[:, 0] = real.reshape(shape)
    out[:, 1] = imag.reshape(shape)


def last_kernel(stack, x, out):
    real, imag = apply_section(stack[...], x[...])
    out[pl.ds(0, ROWS, stride=2), :] = real
    out[pl.ds(1, ROWS, stride=2), :] = imag


SMEM = pl.BlockSpec(memory_space=pltpu.SMEM)
VMEM = pl.BlockSpec(memory_space=pltpu.VMEM)
SCALARS = [pltpu.SMEM((ROW_BITS,), jnp.int32), pltpu.SMEM((ROW_BITS + 1,), jnp.int32)]
UNIT = 2 * DIM**3


def gates_spec(section):
    return pl.BlockSpec((2, 2, DIM, DIM), lambda i: (section, 0, 0, 0))


def cost(units, moved):
    return pl.CostEstimate(flops=units * UNIT, bytes_accessed=moved, transcendentals=0)


def first_section(x, gates, bits, plan, narrow_bits):
    blocks = 2**narrow_bits
    shape = (blocks, 2, ROWS // blocks, LANES)
    return pl.pallas_call(
        functools.partial(first_kernel, narrow_bits),
        grid=(1,),
        out_shape=jax.ShapeDtypeStruct(shape, F32),
        in_specs=[SMEM, SMEM, VMEM, gates_spec(0)],
        out_specs=VMEM,
        scratch_shapes=SCALARS,
        cost_estimate=cost(48, 2 * 2**20),
        name="first_section",
    )(bits, plan, x, gates)


def section_operator(section, gates, bits, plan, order_in, order_out):
    return pl.pallas_call(
        functools.partial(operator_kernel, section, order_in, order_out),
        grid=(1,),
        out_shape=jax.ShapeDtypeStruct((4 * ROWS, ROWS), BF16),
        in_specs=[SMEM, SMEM, gates_spec(section)],
        out_specs=VMEM,
        scratch_shapes=SCALARS,
        cost_estimate=cost(128, 3 * 2**20),
        name="section_operator",
    )(bits, plan, gates)


def run_section(kernel, stack, x, shape, name):
    return pl.pallas_call(
        kernel,
        out_shape=jax.ShapeDtypeStruct(shape, F32),
        in_specs=[VMEM, VMEM],
        out_specs=VMEM,
        cost_estimate=cost(24, 3 * 2**20),
        name=name,
    )(stack, x)


def exchange(blocks, axis):
    flat = blocks.reshape(blocks.shape[0], -1, LANES)
    flat = lax.all_to_all(flat, axis, split_axis=0, concat_axis=0, tiled=True)
    return flat.reshape(blocks.shape)


def shards(state, gates, gate_bits, slot_plan):
    narrow_bits = lax.axis_size("narrow").bit_length() - 1
    wide_bits = lax.axis_size("wide").bit_length() - 1
    x = state.reshape(2, ROWS, LANES).transpose(1, 0, 2).reshape(2 * ROWS, LANES)

    def narrow_order(plan, rest):
        return plan_slots(plan, 0, narrow_bits, rest)

    def wide_order(plan, rest):
        return plan_slots(plan, narrow_bits, wide_bits, rest)

    def natural(plan, rest):
        return list(range(ROW_BITS))

    blocks = first_section(x, gates, gate_bits, slot_plan, narrow_bits)
    second = section_operator(1, gates, gate_bits, slot_plan, narrow_order, wide_order)
    third = section_operator(2, gates, gate_bits, slot_plan, wide_order, natural)
    blocks = exchange(blocks, "narrow")
    wide = 2**wide_bits
    blocks = run_section(
        middle_kernel, second, blocks, (wide, 2, ROWS // wide, LANES), "middle_section"
    )
    blocks = exchange(blocks, "wide")
    x = run_section(last_kernel, third, blocks, (2 * ROWS, LANES), "last_section")
    return x.reshape(ROWS, 2, LANES).transpose(1, 0, 2).reshape(2, ROWS * LANES)


def solution(mesh):
    return jax.shard_map(
        shards,
        mesh=mesh,
        in_specs=(P(None, ("wide", "narrow")), P(), P(), P()),
        out_specs=P(None, ("wide", "narrow")),
        check_vma=False,
    )
```

```python
import functools

import jax
import jax.numpy as jnp
from jax import lax
from jax.experimental import pallas as pl
from jax.experimental.pallas import tpu as pltpu
from jax.sharding import PartitionSpec as P

LANE_BITS = 7
LANES = 2**LANE_BITS
ROW_BITS = 9
ROWS = 2**ROW_BITS
DIM_BITS = 8
DIM = 2**DIM_BITS

BF16 = jnp.bfloat16
F32 = jnp.float32


def mm(a, b):
    return jnp.dot(a, b, preferred_element_type=F32)


def split(x):
    high = x.astype(BF16)
    low = (x - high.astype(F32)).astype(BF16)
    return high, low


def gate_slots(bits, gate):
    used = [bits[gate, j] - LANE_BITS for j in range(DIM_BITS)]
    free = ROW_BITS * (ROW_BITS - 1) // 2 - sum(used)
    return used + [free]


def plan_slots(plan, start, count, rest):
    slots = [plan[start + b] - LANE_BITS for b in range(count)]
    filled = jnp.int32(0)
    for p in range(ROW_BITS):
        rest[filled] = jnp.int32(p)
        taken = functools.reduce(jnp.logical_or, [s == p for s in slots])
        filled = filled + jnp.where(taken, 0, 1).astype(jnp.int32)
    return [rest[k] for k in range(ROW_BITS - count)] + slots


def permutation(source, target, where):
    for place in range(ROW_BITS):
        where[target[place]] = jnp.int32(place)
    lane = lax.broadcasted_iota(jnp.int32, (8, ROWS), 1)
    moved = jnp.zeros((8, ROWS), jnp.int32)
    for place in range(ROW_BITS):
        moved = moved | (((lane >> place) & 1) << where[source[place]])
    row = lax.broadcasted_iota(jnp.int32, (ROWS, ROWS), 0)
    hit = jnp.broadcast_to(moved[:1], (ROWS, ROWS)) == row
    return jnp.where(hit, 1.0, 0.0).astype(BF16)


def stack_gate(real, imag):
    real_high, real_low = split(real)
    imag_high, imag_low = split(imag)
    return jnp.concatenate([real_high, imag_high, real_low, imag_low], axis=0)


def pack_parts(real, imag):
    real_high, real_low = split(real)
    imag_high, imag_low = split(imag)
    return jnp.concatenate([real_high, imag_high, real_low, imag_low], axis=1)


def complex_product(stack, high, low, width):
    half = stack.shape[0] // 2
    quarter = half // 2
    first = mm(stack, high)
    total = first[:half] + first[half:] + mm(stack[:half], low)
    real = total[:quarter, :width] - total[quarter:, width:]
    imag = total[:quarter, width:] + total[quarter:, :width]
    return real, imag


def gate_on_parts(stack, parts, width):
    reals, imags = [], []
    for free in range(2):
        rows = parts[free * DIM : (free + 1) * DIM]
        real, imag = complex_product(stack, rows[:, : 2 * width], rows[:, 2 * width :], width)
        reals.append(real)
        imags.append(imag)
    return jnp.concatenate(reals, axis=0), jnp.concatenate(imags, axis=0)


def first_kernel(narrow_bits, bits, plan, x_hbm, gates_hbm, out, where, rest, x, gates, sems):
    copies = [pltpu.make_async_copy(x_hbm, x, sems.at[0])]
    for gate in range(2):
        copies.append(
            pltpu.make_async_copy(gates_hbm.at[gate], gates.at[gate], sems.at[gate + 1])
        )
    for copy in copies:
        copy.start()
    natural = list(range(ROW_BITS))
    order_a = gate_slots(bits, 0)
    order_b = gate_slots(bits, 1)
    order_out = plan_slots(plan, 0, narrow_bits, rest)
    enter = permutation(natural, order_a, where)
    for copy in copies:
        copy.wait()
    parts = pack_parts(x[pl.ds(0, ROWS, stride=2), :], x[pl.ds(1, ROWS, stride=2), :])
    parts = mm(enter, parts).astype(BF16)
    real, imag = gate_on_parts(stack_gate(gates[0, 0], gates[0, 1]), parts, LANES)
    parts = mm(permutation(order_a, order_b, where), pack_parts(real, imag)).astype(BF16)
    real, imag = gate_on_parts(stack_gate(gates[1, 0], gates[1, 1]), parts, LANES)
    parts = mm(permutation(order_b, order_out, where), pack_parts(real, imag))
    blocks = out.shape[0]
    shape = (blocks, ROWS // blocks, LANES)
    out[:, 0] = (parts[:, :LANES] + parts[:, 2 * LANES : 3 * LANES]).reshape(shape)
    out[:, 1] = (parts[:, LANES : 2 * LANES] + parts[:, 3 * LANES :]).reshape(shape)


def operator_kernel(section, order_in, order_out, bits, plan, gates, out, where, rest):
    order_a = gate_slots(bits, 2 * section)
    order_b = gate_slots(bits, 2 * section + 1)
    columns = order_in(plan, rest)
    result = order_out(plan, rest)
    pick = permutation(columns, order_a, where)
    stack = stack_gate(gates[0, 0], gates[0, 1])
    picked = [mm(stack, pick[free * DIM : (free + 1) * DIM]).astype(BF16) for free in range(2)]
    parts = jnp.concatenate(
        [
            jnp.concatenate([p[k * DIM : (k + 1) * DIM] for p in picked], axis=0)
            for k in range(4)
        ],
        axis=1,
    )
    parts = mm(permutation(order_a, order_b, where), parts).astype(BF16)
    real, imag = gate_on_parts(stack_gate(gates[1, 0], gates[1, 1]), parts, ROWS)
    final = permutation(order_b, result, where)
    for k, part in enumerate([*split(real), *split(imag)]):
        place = (k % 2) * 2 + k // 2
        out[place * ROWS : (place + 1) * ROWS, :] = mm(final, part).astype(BF16)


def apply_section(stack, x):
    real = x[:, 0].reshape(ROWS, LANES)
    imag = x[:, 1].reshape(ROWS, LANES)
    real_high, real_low = split(real)
    imag_high, imag_low = split(imag)
    high = jnp.concatenate([real_high, imag_high], axis=1)
    low = jnp.concatenate([real_low, imag_low], axis=1)
    return complex_product(stack, high, low, LANES)


def middle_kernel(stack, x, out):
    real, imag = apply_section(stack[...], x[...])
    blocks = out.shape[0]
    shape = (blocks, ROWS // blocks, LANES)
    out[:, 0] = real.reshape(shape)
    out[:, 1] = imag.reshape(shape)


def last_kernel(stack, x, out):
    real, imag = apply_section(stack[...], x[...])
    out[pl.ds(0, ROWS, stride=2), :] = real
    out[pl.ds(1, ROWS, stride=2), :] = imag


SMEM = pl.BlockSpec(memory_space=pltpu.SMEM)
VMEM = pl.BlockSpec(memory_space=pltpu.VMEM)
ANY = pl.BlockSpec(memory_space=pl.ANY)
SCALARS = [pltpu.SMEM((ROW_BITS,), jnp.int32), pltpu.SMEM((ROW_BITS + 1,), jnp.int32)]
UNIT = 2 * DIM**3


def gates_spec(section):
    return pl.BlockSpec((2, 2, DIM, DIM), lambda i: (section, 0, 0, 0))


def cost(units, moved):
    return pl.CostEstimate(flops=units * UNIT, bytes_accessed=moved, transcendentals=0)


def first_section(x, gates, bits, plan, narrow_bits):
    blocks = 2**narrow_bits
    shape = (blocks, 2, ROWS // blocks, LANES)
    return pl.pallas_call(
        functools.partial(first_kernel, narrow_bits),
        out_shape=vmem_shape(shape, F32),
        in_specs=[SMEM, SMEM, ANY, ANY],
        out_specs=VMEM,
        scratch_shapes=[
            *SCALARS,
            pltpu.VMEM(x.shape, F32),
            pltpu.VMEM((2, *gates.shape[1:]), F32),
            pltpu.SemaphoreType.DMA((3,)),
        ],
        cost_estimate=cost(48, 2 * 2**20),
        name="first_section",
    )(bits, plan, x, gates)


def section_operator(section, gates, bits, plan, order_in, order_out):
    return pl.pallas_call(
        functools.partial(operator_kernel, section, order_in, order_out),
        grid=(1,),
        out_shape=vmem_shape((4 * ROWS, ROWS), BF16),
        in_specs=[SMEM, SMEM, gates_spec(section)],
        out_specs=VMEM,
        scratch_shapes=SCALARS,
        cost_estimate=cost(128, 3 * 2**20),
        name="section_operator",
    )(bits, plan, gates)


def vmem_shape(shape, dtype):
    return pltpu.VMEM(shape, dtype)


def in_vmem(x):
    return pltpu.with_memory_space_constraint(x, pltpu.VMEM)


def run_section(kernel, stack, x, out_shape, name):
    return pl.pallas_call(
        kernel,
        out_shape=out_shape,
        in_specs=[VMEM, VMEM],
        out_specs=VMEM,
        cost_estimate=cost(24, 3 * 2**20),
        name=name,
    )(in_vmem(stack), in_vmem(x))


def exchange(blocks, axis):
    flat = blocks.reshape(blocks.shape[0], -1, LANES)
    flat = lax.all_to_all(flat, axis, split_axis=0, concat_axis=0, tiled=True)
    return flat.reshape(blocks.shape)


def shards(state, gates, gate_bits, slot_plan):
    narrow_bits = lax.axis_size("narrow").bit_length() - 1
    wide_bits = lax.axis_size("wide").bit_length() - 1
    x = state.reshape(2, ROWS, LANES).transpose(1, 0, 2).reshape(2 * ROWS, LANES)

    def narrow_order(plan, rest):
        return plan_slots(plan, 0, narrow_bits, rest)

    def wide_order(plan, rest):
        return plan_slots(plan, narrow_bits, wide_bits, rest)

    def natural(plan, rest):
        return list(range(ROW_BITS))

    blocks = first_section(x, gates, gate_bits, slot_plan, narrow_bits)
    second = section_operator(1, gates, gate_bits, slot_plan, narrow_order, wide_order)
    third = section_operator(2, gates, gate_bits, slot_plan, wide_order, natural)
    blocks = exchange(blocks, "narrow")
    wide = 2**wide_bits
    shape = vmem_shape((wide, 2, ROWS // wide, LANES), F32)
    blocks = run_section(middle_kernel, second, blocks, shape, "middle_section")
    blocks = exchange(blocks, "wide")
    shape = jax.ShapeDtypeStruct((2 * ROWS, LANES), F32)
    x = run_section(last_kernel, third, blocks, shape, "last_section")
    return x.reshape(ROWS, 2, LANES).transpose(1, 0, 2).reshape(2, ROWS * LANES)


def solution(mesh):
    return jax.shard_map(
        shards,
        mesh=mesh,
        in_specs=(P(None, ("wide", "narrow")), P(), P(), P()),
        out_specs=P(None, ("wide", "narrow")),
        check_vma=False,
    )
```

```python
import functools

import jax
import jax.numpy as jnp
from jax import lax
from jax.experimental import pallas as pl
from jax.experimental.pallas import tpu as pltpu
from jax.sharding import PartitionSpec as P

LANE_BITS = 7
LANES = 2**LANE_BITS
ROW_BITS = 9
ROWS = 2**ROW_BITS
DIM_BITS = 8
DIM = 2**DIM_BITS

BF16 = jnp.bfloat16
F32 = jnp.float32


def mm(a, b):
    return jnp.dot(a, b, preferred_element_type=F32)


def split(x):
    high = x.astype(BF16)
    low = (x - high.astype(F32)).astype(BF16)
    return high, low


def gate_slots(bits, gate):
    used = [bits[gate, j] - LANE_BITS for j in range(DIM_BITS)]
    free = ROW_BITS * (ROW_BITS - 1) // 2 - sum(used)
    return used + [free]


def plan_slots(plan, start, count, rest):
    slots = [plan[start + b] - LANE_BITS for b in range(count)]
    filled = jnp.int32(0)
    for p in range(ROW_BITS):
        rest[filled] = jnp.int32(p)
        taken = functools.reduce(jnp.logical_or, [s == p for s in slots])
        filled = filled + jnp.where(taken, 0, 1).astype(jnp.int32)
    return [rest[k] for k in range(ROW_BITS - count)] + slots


def permutation(source, target, where):
    for place in range(ROW_BITS):
        where[target[place]] = jnp.int32(place)
    lane = lax.broadcasted_iota(jnp.int32, (8, ROWS), 1)
    moved = jnp.zeros((8, ROWS), jnp.int32)
    for place in range(ROW_BITS):
        moved = moved | (((lane >> place) & 1) << where[source[place]])
    row = lax.broadcasted_iota(jnp.int32, (ROWS, ROWS), 0)
    hit = jnp.broadcast_to(moved[:1], (ROWS, ROWS)) == row
    return jnp.where(hit, 1.0, 0.0).astype(BF16)


def stack_gate(real, imag):
    real_high, real_low = split(real)
    imag_high, imag_low = split(imag)
    return jnp.concatenate([real_high, imag_high, real_low, imag_low], axis=0)


def pack_parts(real, imag):
    real_high, real_low = split(real)
    imag_high, imag_low = split(imag)
    return jnp.concatenate([real_high, imag_high, real_low, imag_low], axis=1)


def complex_product(stack, high, low, width):
    half = stack.shape[0] // 2
    quarter = half // 2
    first = mm(stack, high)
    total = first[:half] + first[half:] + mm(stack[:half], low)
    real = total[:quarter, :width] - total[quarter:, width:]
    imag = total[:quarter, width:] + total[quarter:, :width]
    return real, imag


def gate_on_parts(stack, parts, width):
    reals, imags = [], []
    for free in range(2):
        rows = parts[free * DIM : (free + 1) * DIM]
        real, imag = complex_product(stack, rows[:, : 2 * width], rows[:, 2 * width :], width)
        reals.append(real)
        imags.append(imag)
    return jnp.concatenate(reals, axis=0), jnp.concatenate(imags, axis=0)


def first_kernel(narrow_bits, bits, plan, x, gates, out, where, rest):
    natural = list(range(ROW_BITS))
    order_a = gate_slots(bits, 0)
    order_b = gate_slots(bits, 1)
    order_out = plan_slots(plan, 0, narrow_bits, rest)
    parts = pack_parts(x[pl.ds(0, ROWS, stride=2), :], x[pl.ds(1, ROWS, stride=2), :])
    parts = mm(permutation(natural, order_a, where), parts).astype(BF16)
    real, imag = gate_on_parts(stack_gate(gates[0, 0], gates[0, 1]), parts, LANES)
    parts = pack_parts(real, imag)
    parts = mm(permutation(order_a, order_b, where), parts).astype(BF16)
    real, imag = gate_on_parts(stack_gate(gates[1, 0], gates[1, 1]), parts, LANES)
    parts = mm(permutation(order_b, order_out, where), pack_parts(real, imag))
    blocks = out.shape[0]
    shape = (blocks, ROWS // blocks, LANES)
    out[:, 0] = (parts[:, :LANES] + parts[:, 2 * LANES : 3 * LANES]).reshape(shape)
    out[:, 1] = (parts[:, LANES : 2 * LANES] + parts[:, 3 * LANES :]).reshape(shape)


def operator_kernel(section, order_in, order_out, bits, plan, gates, out, where, rest):
    order_a = gate_slots(bits, 2 * section)
    order_b = gate_slots(bits, 2 * section + 1)
    columns = order_in(plan, rest)
    result = order_out(plan, rest)
    pick = permutation(columns, order_a, where)
    stack = stack_gate(gates[0, 0], gates[0, 1])
    picked = [mm(stack, pick[free * DIM : (free + 1) * DIM]).astype(BF16) for free in range(2)]
    parts = jnp.concatenate(
        [
            jnp.concatenate([p[k * DIM : (k + 1) * DIM] for p in picked], axis=0)
            for k in range(4)
        ],
        axis=1,
    )
    parts = mm(permutation(order_a, order_b, where), parts).astype(BF16)
    real, imag = gate_on_parts(stack_gate(gates[1, 0], gates[1, 1]), parts, ROWS)
    final = permutation(order_b, result, where)
    for k, part in enumerate([*split(real), *split(imag)]):
        place = (k % 2) * 2 + k // 2
        out[place * ROWS : (place + 1) * ROWS, :] = mm(final, part).astype(BF16)


def apply_section(stack, x):
    real = x[:, 0].reshape(ROWS, LANES)
    imag = x[:, 1].reshape(ROWS, LANES)
    real_high, real_low = split(real)
    imag_high, imag_low = split(imag)
    high = jnp.concatenate([real_high, imag_high], axis=1)
    low = jnp.concatenate([real_low, imag_low], axis=1)
    return complex_product(stack, high, low, LANES)


def middle_kernel(stack, x, out):
    real, imag = apply_section(stack[...], x[...])
    blocks = out.shape[0]
    shape = (blocks, ROWS // blocks, LANES)
    out[:, 0] = real.reshape(shape)
    out[:, 1] = imag.reshape(shape)


def last_kernel(stack, x, out):
    real, imag = apply_section(stack[...], x[...])
    out[pl.ds(0, ROWS, stride=2), :] = real
    out[pl.ds(1, ROWS, stride=2), :] = imag


SMEM = pl.BlockSpec(memory_space=pltpu.SMEM)
VMEM = pl.BlockSpec(memory_space=pltpu.VMEM)
SCALARS = [pltpu.SMEM((ROW_BITS,), jnp.int32), pltpu.SMEM((ROW_BITS + 1,), jnp.int32)]
UNIT = 2 * DIM**3


def gates_spec(section):
    return pl.BlockSpec((2, 2, DIM, DIM), lambda i: (section, 0, 0, 0))


def cost(units, moved):
    return pl.CostEstimate(flops=units * UNIT, bytes_accessed=moved, transcendentals=0)


def first_section(x, gates, bits, plan, narrow_bits):
    blocks = 2**narrow_bits
    shape = (blocks, 2, ROWS // blocks, LANES)
    return pl.pallas_call(
        functools.partial(first_kernel, narrow_bits),
        grid=(1,),
        out_shape=vmem_shape(shape, F32),
        in_specs=[SMEM, SMEM, VMEM, gates_spec(0)],
        out_specs=VMEM,
        scratch_shapes=SCALARS,
        cost_estimate=cost(48, 2 * 2**20),
        name="first_section",
    )(bits, plan, x, gates)


def section_operator(section, gates, bits, plan, order_in, order_out):
    return pl.pallas_call(
        functools.partial(operator_kernel, section, order_in, order_out),
        grid=(1,),
        out_shape=vmem_shape((4 * ROWS, ROWS), BF16),
        in_specs=[SMEM, SMEM, gates_spec(section)],
        out_specs=VMEM,
        scratch_shapes=SCALARS,
        cost_estimate=cost(128, 3 * 2**20),
        name="section_operator",
    )(bits, plan, gates)


def vmem_shape(shape, dtype):
    return pltpu.VMEM(shape, dtype)


def in_vmem(x):
    return pltpu.with_memory_space_constraint(x, pltpu.VMEM)


def run_section(kernel, stack, x, out_shape, name):
    return pl.pallas_call(
        kernel,
        out_shape=out_shape,
        in_specs=[VMEM, VMEM],
        out_specs=VMEM,
        cost_estimate=cost(24, 3 * 2**20),
        name=name,
    )(in_vmem(stack), in_vmem(x))


def exchange(blocks, axis):
    flat = blocks.reshape(blocks.shape[0], -1, LANES)
    flat = lax.all_to_all(flat, axis, split_axis=0, concat_axis=0, tiled=True)
    return flat.reshape(blocks.shape)


def shards(state, gates, gate_bits, slot_plan):
    narrow_bits = lax.axis_size("narrow").bit_length() - 1
    wide_bits = lax.axis_size("wide").bit_length() - 1
    x = state.reshape(2, ROWS, LANES).transpose(1, 0, 2).reshape(2 * ROWS, LANES)

    def narrow_order(plan, rest):
        return plan_slots(plan, 0, narrow_bits, rest)

    def wide_order(plan, rest):
        return plan_slots(plan, narrow_bits, wide_bits, rest)

    def natural(plan, rest):
        return list(range(ROW_BITS))

    blocks = first_section(x, gates, gate_bits, slot_plan, narrow_bits)
    second = section_operator(1, gates, gate_bits, slot_plan, narrow_order, wide_order)
    third = section_operator(2, gates, gate_bits, slot_plan, wide_order, natural)
    blocks = exchange(blocks, "narrow")
    wide = 2**wide_bits
    shape = vmem_shape((wide, 2, ROWS // wide, LANES), F32)
    blocks = run_section(middle_kernel, second, blocks, shape, "middle_section")
    blocks = exchange(blocks, "wide")
    shape = jax.ShapeDtypeStruct((2 * ROWS, LANES), F32)
    x = run_section(last_kernel, third, blocks, shape, "last_section")
    return x.reshape(ROWS, 2, LANES).transpose(1, 0, 2).reshape(2, ROWS * LANES)


def solution(mesh):
    return jax.shard_map(
        shards,
        mesh=mesh,
        in_specs=(P(None, ("wide", "narrow")), P(), P(), P()),
        out_specs=P(None, ("wide", "narrow")),
        check_vma=False,
    )
```

```python
import functools

import jax
import jax.numpy as jnp
from jax import lax
from jax.experimental import pallas as pl
from jax.experimental.pallas import tpu as pltpu
from jax.sharding import PartitionSpec as P

LANE_BITS = 7
LANES = 2**LANE_BITS
ROW_BITS = 9
ROWS = 2**ROW_BITS
DIM_BITS = 8
DIM = 2**DIM_BITS

BF16 = jnp.bfloat16
F32 = jnp.float32


def mm(a, b):
    return jnp.dot(a, b, preferred_element_type=F32)


def split(x):
    high = x.astype(BF16)
    low = (x - high.astype(F32)).astype(BF16)
    return high, low


def gate_slots(bits, gate):
    used = [bits[gate, j] - LANE_BITS for j in range(DIM_BITS)]
    free = ROW_BITS * (ROW_BITS - 1) // 2 - sum(used)
    return used + [free]


def plan_slots(plan, start, count, rest, turned=None):
    slots = [plan[start + b] - LANE_BITS for b in range(count)]
    if turned is not None:
        half = count // 2
        slots = [jnp.where(turned == 1, plan[start + (b + half) % count], plan[start + b]) for b in range(count)]
        slots = [slot - LANE_BITS for slot in slots]
    filled = jnp.int32(0)
    for p in range(ROW_BITS):
        rest[filled] = jnp.int32(p)
        taken = functools.reduce(jnp.logical_or, [s == p for s in slots])
        filled = filled + jnp.where(taken, 0, 1).astype(jnp.int32)
    return [rest[k] for k in range(ROW_BITS - count)] + slots


def permutation(source, target, where):
    for place in range(ROW_BITS):
        where[target[place]] = jnp.int32(place)
    lane = lax.broadcasted_iota(jnp.int32, (8, ROWS), 1)
    moved = jnp.zeros((8, ROWS), jnp.int32)
    for place in range(ROW_BITS):
        moved = moved | (((lane >> place) & 1) << where[source[place]])
    row = lax.broadcasted_iota(jnp.int32, (ROWS, ROWS), 0)
    hit = jnp.broadcast_to(moved[:1], (ROWS, ROWS)) == row
    return jnp.where(hit, 1.0, 0.0).astype(BF16)


def stack_gate(real, imag):
    real_high, real_low = split(real)
    imag_high, imag_low = split(imag)
    return jnp.concatenate([real_high, imag_high, real_low, imag_low], axis=0)


def pack_parts(real, imag):
    real_high, real_low = split(real)
    imag_high, imag_low = split(imag)
    return jnp.concatenate([real_high, imag_high, real_low, imag_low], axis=1)


def complex_product(stack, high, low, width):
    half = stack.shape[0] // 2
    quarter = half // 2
    first = mm(stack, high)
    total = first[:half] + first[half:] + mm(stack[:half], low)
    real = total[:quarter, :width] - total[quarter:, width:]
    imag = total[:quarter, width:] + total[quarter:, :width]
    return real, imag


def gate_on_parts(stack, parts, width):
    reals, imags = [], []
    for free in range(2):
        rows = parts[free * DIM : (free + 1) * DIM]
        real, imag = complex_product(stack, rows[:, : 2 * width], rows[:, 2 * width :], width)
        reals.append(real)
        imags.append(imag)
    return jnp.concatenate(reals, axis=0), jnp.concatenate(imags, axis=0)


def first_kernel(narrow_bits, bits, plan, x, gates, out, where, rest):
    natural = list(range(ROW_BITS))
    order_a = gate_slots(bits, 0)
    order_b = gate_slots(bits, 1)
    order_out = plan_slots(plan, 0, narrow_bits, rest)
    parts = pack_parts(x[pl.ds(0, ROWS, stride=2), :], x[pl.ds(1, ROWS, stride=2), :])
    parts = mm(permutation(natural, order_a, where), parts).astype(BF16)
    real, imag = gate_on_parts(stack_gate(gates[0, 0], gates[0, 1]), parts, LANES)
    parts = pack_parts(real, imag)
    parts = mm(permutation(order_a, order_b, where), parts).astype(BF16)
    real, imag = gate_on_parts(stack_gate(gates[1, 0], gates[1, 1]), parts, LANES)
    parts = mm(permutation(order_b, order_out, where), pack_parts(real, imag))
    blocks = out.shape[0]
    shape = (blocks, ROWS // blocks, LANES)
    out[:, 0] = (parts[:, :LANES] + parts[:, 2 * LANES : 3 * LANES]).reshape(shape)
    out[:, 1] = (parts[:, LANES : 2 * LANES] + parts[:, 3 * LANES :]).reshape(shape)


def operator_kernel(section, order_in, order_out, bits, plan, core, gates, out, where, rest):
    order_a = gate_slots(bits, 2 * section)
    order_b = gate_slots(bits, 2 * section + 1)
    columns = order_in(plan, rest, core[0])
    result = order_out(plan, rest, core[0])
    pick = permutation(columns, order_a, where)
    stack = stack_gate(gates[0, 0], gates[0, 1])
    picked = [mm(stack, pick[free * DIM : (free + 1) * DIM]).astype(BF16) for free in range(2)]
    parts = jnp.concatenate(
        [
            jnp.concatenate([p[k * DIM : (k + 1) * DIM] for p in picked], axis=0)
            for k in range(4)
        ],
        axis=1,
    )
    parts = mm(permutation(order_a, order_b, where), parts).astype(BF16)
    real, imag = gate_on_parts(stack_gate(gates[1, 0], gates[1, 1]), parts, ROWS)
    final = permutation(order_b, result, where)
    for k, part in enumerate([*split(real), *split(imag)]):
        place = (k % 2) * 2 + k // 2
        out[place * ROWS : (place + 1) * ROWS, :] = mm(final, part).astype(BF16)


def apply_section(stack, x):
    real = x[:, 0].reshape(ROWS, LANES)
    imag = x[:, 1].reshape(ROWS, LANES)
    real_high, real_low = split(real)
    imag_high, imag_low = split(imag)
    high = jnp.concatenate([real_high, imag_high], axis=1)
    low = jnp.concatenate([real_low, imag_low], axis=1)
    return complex_product(stack, high, low, LANES)


def middle_kernel(stack, x, out):
    real, imag = apply_section(stack[...], x[...])
    blocks = out.shape[0]
    shape = (blocks, ROWS // blocks, LANES)
    out[:, 0] = real.reshape(shape)
    out[:, 1] = imag.reshape(shape)


def last_kernel(stack, x, out):
    real, imag = apply_section(stack[...], x[...])
    out[pl.ds(0, ROWS, stride=2), :] = real
    out[pl.ds(1, ROWS, stride=2), :] = imag


SMEM = pl.BlockSpec(memory_space=pltpu.SMEM)
VMEM = pl.BlockSpec(memory_space=pltpu.VMEM)
SCALARS = [pltpu.SMEM((ROW_BITS,), jnp.int32), pltpu.SMEM((ROW_BITS + 1,), jnp.int32)]
UNIT = 2 * DIM**3


def gates_spec(section):
    return pl.BlockSpec((2, 2, DIM, DIM), lambda i: (section, 0, 0, 0))


def cost(units, moved):
    return pl.CostEstimate(flops=units * UNIT, bytes_accessed=moved, transcendentals=0)


def first_section(x, gates, bits, plan, narrow_bits):
    blocks = 2**narrow_bits
    shape = (blocks, 2, ROWS // blocks, LANES)
    return pl.pallas_call(
        functools.partial(first_kernel, narrow_bits),
        grid=(1,),
        out_shape=vmem_shape(shape, F32),
        in_specs=[SMEM, SMEM, VMEM, gates_spec(0)],
        out_specs=VMEM,
        scratch_shapes=SCALARS,
        cost_estimate=cost(48, 2 * 2**20),
        name="first_section",
    )(bits, plan, x, gates)


def section_operator(section, gates, bits, plan, core, order_in, order_out):
    return pl.pallas_call(
        functools.partial(operator_kernel, section, order_in, order_out),
        grid=(1,),
        out_shape=vmem_shape((4 * ROWS, ROWS), BF16),
        in_specs=[SMEM, SMEM, SMEM, gates_spec(section)],
        out_specs=VMEM,
        scratch_shapes=SCALARS,
        cost_estimate=cost(128, 3 * 2**20),
        name="section_operator",
    )(bits, plan, core, gates)


def vmem_shape(shape, dtype):
    return pltpu.VMEM(shape, dtype)


def in_vmem(x):
    return pltpu.with_memory_space_constraint(x, pltpu.VMEM)


def run_section(kernel, stack, x, out_shape, name):
    return pl.pallas_call(
        kernel,
        out_shape=out_shape,
        in_specs=[VMEM, VMEM],
        out_specs=VMEM,
        cost_estimate=cost(24, 3 * 2**20),
        name=name,
    )(in_vmem(stack), in_vmem(x))


def exchange_narrow(blocks):
    flat = blocks.reshape(blocks.shape[0], -1, LANES)
    flat = lax.all_to_all(flat, "narrow", split_axis=0, concat_axis=0, tiled=True)
    return flat.reshape(blocks.shape)


def wide_groups(wide, narrow, high_on_even):
    side = 2 ** ((wide.bit_length() - 1) // 2)
    other = wide // side
    groups = []
    for n in range(narrow):
        if (n % 2 == 0) == high_on_even:
            groups += [[(j * side + k) * narrow + n for j in range(other)] for k in range(side)]
        else:
            groups += [[(k * side + j) * narrow + n for j in range(side)] for k in range(other)]
    return groups


def exchange_wide(blocks, wide, narrow):
    side = 2 ** ((wide.bit_length() - 1) // 2)
    square = blocks.reshape(side, side, -1, LANES)
    for turn in range(2):
        if turn:
            square = square.transpose(1, 0, 2, 3)
        square = lax.all_to_all(
            square,
            ("wide", "narrow"),
            split_axis=0,
            concat_axis=0,
            tiled=True,
            axis_index_groups=wide_groups(wide, narrow, turn == 0),
        )
    return square.reshape(blocks.shape)


def shards(state, gates, gate_bits, slot_plan):
    narrow = lax.axis_size("narrow")
    wide = lax.axis_size("wide")
    narrow_bits = narrow.bit_length() - 1
    wide_bits = wide.bit_length() - 1
    core = (lax.axis_index("narrow") % 2).astype(jnp.int32).reshape(1)
    x = state.reshape(2, ROWS, LANES).transpose(1, 0, 2).reshape(2 * ROWS, LANES)

    def narrow_order(plan, rest, core):
        return plan_slots(plan, 0, narrow_bits, rest)

    def wide_order(plan, rest, core):
        return plan_slots(plan, narrow_bits, wide_bits, rest, core)

    def turned_order(plan, rest, core):
        return plan_slots(plan, narrow_bits, wide_bits, rest, 1 - core)

    def natural(plan, rest, core):
        return list(range(ROW_BITS))

    blocks = first_section(x, gates, gate_bits, slot_plan, narrow_bits)
    second = section_operator(1, gates, gate_bits, slot_plan, core, narrow_order, wide_order)
    third = section_operator(2, gates, gate_bits, slot_plan, core, turned_order, natural)
    blocks = exchange_narrow(blocks)
    shape = vmem_shape((wide, 2, ROWS // wide, LANES), F32)
    blocks = run_section(middle_kernel, second, blocks, shape, "middle_section")
    blocks = exchange_wide(blocks, wide, narrow)
    shape = jax.ShapeDtypeStruct((2 * ROWS, LANES), F32)
    x = run_section(last_kernel, third, blocks, shape, "last_section")
    return x.reshape(ROWS, 2, LANES).transpose(1, 0, 2).reshape(2, ROWS * LANES)


def solution(mesh):
    return jax.shard_map(
        shards,
        mesh=mesh,
        in_specs=(P(None, ("wide", "narrow")), P(), P(), P()),
        out_specs=P(None, ("wide", "narrow")),
        check_vma=False,
    )
```

```python
import functools

import jax
import jax.numpy as jnp
from jax import lax
from jax.experimental import pallas as pl
from jax.experimental.pallas import tpu as pltpu
from jax.sharding import PartitionSpec as P

LANE_BITS = 7
LANES = 2**LANE_BITS
ROW_BITS = 9
ROWS = 2**ROW_BITS
DIM_BITS = 8
DIM = 2**DIM_BITS

BF16 = jnp.bfloat16
F32 = jnp.float32


def mm(a, b):
    return jnp.dot(a, b, preferred_element_type=F32)


def split(x):
    high = x.astype(BF16)
    low = (x - high.astype(F32)).astype(BF16)
    return high, low


def gate_slots(bits, gate):
    used = [bits[gate, j] - LANE_BITS for j in range(DIM_BITS)]
    free = ROW_BITS * (ROW_BITS - 1) // 2 - sum(used)
    return used + [free]


def plan_slots(plan, start, count, rest, turned=None):
    slots = [plan[start + b] - LANE_BITS for b in range(count)]
    if turned is not None:
        half = count // 2
        slots = [jnp.where(turned == 1, plan[start + (b + half) % count], plan[start + b]) for b in range(count)]
        slots = [slot - LANE_BITS for slot in slots]
    filled = jnp.int32(0)
    for p in range(ROW_BITS):
        rest[filled] = jnp.int32(p)
        taken = functools.reduce(jnp.logical_or, [s == p for s in slots])
        filled = filled + jnp.where(taken, 0, 1).astype(jnp.int32)
    return [rest[k] for k in range(ROW_BITS - count)] + slots


def permutation(source, target, where):
    for place in range(ROW_BITS):
        where[target[place]] = jnp.int32(place)
    lane = lax.broadcasted_iota(jnp.int32, (8, ROWS), 1)
    moved = jnp.zeros((8, ROWS), jnp.int32)
    for place in range(ROW_BITS):
        moved = moved | (((lane >> place) & 1) << where[source[place]])
    row = lax.broadcasted_iota(jnp.int32, (ROWS, ROWS), 0)
    hit = jnp.broadcast_to(moved[:1], (ROWS, ROWS)) == row
    return jnp.where(hit, 1.0, 0.0).astype(BF16)


def stack_gate(real, imag):
    real_high, real_low = split(real)
    imag_high, imag_low = split(imag)
    return jnp.concatenate([real_high, imag_high, real_low, imag_low], axis=0)


def pack_parts(real, imag):
    real_high, real_low = split(real)
    imag_high, imag_low = split(imag)
    return jnp.concatenate([real_high, imag_high, real_low, imag_low], axis=1)


def complex_product(stack, high, low, width):
    half = stack.shape[0] // 2
    quarter = half // 2
    first = mm(stack, high)
    total = first[:half] + first[half:] + mm(stack[:half], low)
    real = total[:quarter, :width] - total[quarter:, width:]
    imag = total[:quarter, width:] + total[quarter:, :width]
    return real, imag


def gate_on_parts(stack, parts, width):
    reals, imags = [], []
    for free in range(2):
        rows = parts[free * DIM : (free + 1) * DIM]
        real, imag = complex_product(stack, rows[:, : 2 * width], rows[:, 2 * width :], width)
        reals.append(real)
        imags.append(imag)
    return jnp.concatenate(reals, axis=0), jnp.concatenate(imags, axis=0)


def first_kernel(narrow_bits, bits, plan, x, gates, out, where, rest):
    natural = list(range(ROW_BITS))
    order_a = gate_slots(bits, 0)
    order_b = gate_slots(bits, 1)
    order_out = plan_slots(plan, 0, narrow_bits, rest)
    parts = pack_parts(x[pl.ds(0, ROWS, stride=2), :], x[pl.ds(1, ROWS, stride=2), :])
    parts = mm(permutation(natural, order_a, where), parts).astype(BF16)
    real, imag = gate_on_parts(stack_gate(gates[0, 0], gates[0, 1]), parts, LANES)
    parts = pack_parts(real, imag)
    parts = mm(permutation(order_a, order_b, where), parts).astype(BF16)
    real, imag = gate_on_parts(stack_gate(gates[1, 0], gates[1, 1]), parts, LANES)
    parts = mm(permutation(order_b, order_out, where), pack_parts(real, imag))
    blocks = out.shape[0]
    shape = (blocks, ROWS // blocks, LANES)
    out[:, 0] = (parts[:, :LANES] + parts[:, 2 * LANES : 3 * LANES]).reshape(shape)
    out[:, 1] = (parts[:, LANES : 2 * LANES] + parts[:, 3 * LANES :]).reshape(shape)


def operator_kernel(section, order_in, order_out, bits, plan, core, gates, out, where, rest):
    order_a = gate_slots(bits, 2 * section)
    order_b = gate_slots(bits, 2 * section + 1)
    columns = order_in(plan, rest, core[0])
    result = order_out(plan, rest, core[0])
    pick = permutation(columns, order_a, where)
    stack = stack_gate(gates[0, 0], gates[0, 1])
    picked = [mm(stack, pick[free * DIM : (free + 1) * DIM]).astype(BF16) for free in range(2)]
    parts = jnp.concatenate(
        [
            jnp.concatenate([p[k * DIM : (k + 1) * DIM] for p in picked], axis=0)
            for k in range(4)
        ],
        axis=1,
    )
    parts = mm(permutation(order_a, order_b, where), parts).astype(BF16)
    real, imag = gate_on_parts(stack_gate(gates[1, 0], gates[1, 1]), parts, ROWS)
    final = permutation(order_b, result, where)
    for k, part in enumerate([*split(real), *split(imag)]):
        place = (k % 2) * 2 + k // 2
        out[place * ROWS : (place + 1) * ROWS, :] = mm(final, part).astype(BF16)


def apply_section(stack, x):
    real = x[:, 0].reshape(ROWS, LANES)
    imag = x[:, 1].reshape(ROWS, LANES)
    real_high, real_low = split(real)
    imag_high, imag_low = split(imag)
    high = jnp.concatenate([real_high, imag_high], axis=1)
    low = jnp.concatenate([real_low, imag_low], axis=1)
    return complex_product(stack, high, low, LANES)


def middle_kernel(stack, x, out):
    real, imag = apply_section(stack[...], x[...])
    blocks = out.shape[0]
    shape = (blocks, ROWS // blocks, LANES)
    out[:, 0] = real.reshape(shape)
    out[:, 1] = imag.reshape(shape)


def last_kernel(stack, x, out):
    real, imag = apply_section(stack[...], x[...])
    out[pl.ds(0, ROWS, stride=2), :] = real
    out[pl.ds(1, ROWS, stride=2), :] = imag


SMEM = pl.BlockSpec(memory_space=pltpu.SMEM)
VMEM = pl.BlockSpec(memory_space=pltpu.VMEM)
SCALARS = [pltpu.SMEM((ROW_BITS,), jnp.int32), pltpu.SMEM((ROW_BITS + 1,), jnp.int32)]
UNIT = 2 * DIM**3


def gates_spec(section):
    return pl.BlockSpec((2, 2, DIM, DIM), lambda i: (section, 0, 0, 0))


def cost(units, moved):
    return pl.CostEstimate(flops=units * UNIT, bytes_accessed=moved, transcendentals=0)


def first_section(x, gates, bits, plan, narrow_bits):
    blocks = 2**narrow_bits
    shape = (blocks, 2, ROWS // blocks, LANES)
    return pl.pallas_call(
        functools.partial(first_kernel, narrow_bits),
        grid=(1,),
        out_shape=vmem_shape(shape, F32),
        in_specs=[SMEM, SMEM, VMEM, gates_spec(0)],
        out_specs=VMEM,
        scratch_shapes=SCALARS,
        cost_estimate=cost(48, 2 * 2**20),
        name="first_section",
    )(bits, plan, x, gates)


def section_operator(section, gates, bits, plan, core, order_in, order_out):
    return pl.pallas_call(
        functools.partial(operator_kernel, section, order_in, order_out),
        grid=(1,),
        out_shape=vmem_shape((4 * ROWS, ROWS), BF16),
        in_specs=[SMEM, SMEM, SMEM, gates_spec(section)],
        out_specs=VMEM,
        scratch_shapes=SCALARS,
        cost_estimate=cost(128, 3 * 2**20),
        compiler_params=pltpu.CompilerParams(vmem_limit_bytes=40 * 2**20),
        name="section_operator",
    )(bits, plan, core, gates)


def vmem_shape(shape, dtype):
    return pltpu.VMEM(shape, dtype)


def in_vmem(x):
    return pltpu.with_memory_space_constraint(x, pltpu.VMEM)


def run_section(kernel, stack, x, out_shape, name):
    return pl.pallas_call(
        kernel,
        out_shape=out_shape,
        in_specs=[VMEM, VMEM],
        out_specs=VMEM,
        cost_estimate=cost(24, 3 * 2**20),
        name=name,
    )(in_vmem(stack), in_vmem(x))


def exchange_narrow(blocks):
    flat = blocks.reshape(blocks.shape[0], -1, LANES)
    flat = lax.all_to_all(flat, "narrow", split_axis=0, concat_axis=0, tiled=True)
    return flat.reshape(blocks.shape)


def wide_groups(wide, narrow, high_on_even):
    side = 2 ** ((wide.bit_length() - 1) // 2)
    other = wide // side
    groups = []
    for n in range(narrow):
        if (n % 2 == 0) == high_on_even:
            groups += [[(j * side + k) * narrow + n for j in range(other)] for k in range(side)]
        else:
            groups += [[(k * side + j) * narrow + n for j in range(side)] for k in range(other)]
    return groups


def exchange_wide(blocks, wide, narrow):
    side = 2 ** ((wide.bit_length() - 1) // 2)
    square = blocks.reshape(side, side, -1, LANES)
    for turn in range(2):
        if turn:
            square = square.transpose(1, 0, 2, 3)
        square = lax.all_to_all(
            square,
            ("wide", "narrow"),
            split_axis=0,
            concat_axis=0,
            tiled=True,
            axis_index_groups=wide_groups(wide, narrow, turn == 0),
        )
    return square.reshape(blocks.shape)


def shards(state, gates, gate_bits, slot_plan):
    narrow = lax.axis_size("narrow")
    wide = lax.axis_size("wide")
    narrow_bits = narrow.bit_length() - 1
    wide_bits = wide.bit_length() - 1
    core = (lax.axis_index("narrow") % 2).astype(jnp.int32).reshape(1)
    x = state.reshape(2, ROWS, LANES).transpose(1, 0, 2).reshape(2 * ROWS, LANES)

    def narrow_order(plan, rest, core):
        return plan_slots(plan, 0, narrow_bits, rest)

    def wide_order(plan, rest, core):
        return plan_slots(plan, narrow_bits, wide_bits, rest, core)

    def turned_order(plan, rest, core):
        return plan_slots(plan, narrow_bits, wide_bits, rest, 1 - core)

    def natural(plan, rest, core):
        return list(range(ROW_BITS))

    blocks = first_section(x, gates, gate_bits, slot_plan, narrow_bits)
    second = section_operator(1, gates, gate_bits, slot_plan, core, narrow_order, wide_order)
    third = section_operator(2, gates, gate_bits, slot_plan, core, turned_order, natural)
    second, third = lax.optimization_barrier((second, third))
    blocks = exchange_narrow(blocks)
    shape = vmem_shape((wide, 2, ROWS // wide, LANES), F32)
    blocks = run_section(middle_kernel, second, blocks, shape, "middle_section")
    blocks = exchange_wide(blocks, wide, narrow)
    shape = jax.ShapeDtypeStruct((2 * ROWS, LANES), F32)
    x = run_section(last_kernel, third, blocks, shape, "last_section")
    return x.reshape(ROWS, 2, LANES).transpose(1, 0, 2).reshape(2, ROWS * LANES)


def solution(mesh):
    return jax.shard_map(
        shards,
        mesh=mesh,
        in_specs=(P(None, ("wide", "narrow")), P(), P(), P()),
        out_specs=P(None, ("wide", "narrow")),
        check_vma=False,
    )
```

```python
import functools

import jax
import jax.numpy as jnp
from jax import lax
from jax.experimental import pallas as pl
from jax.experimental.pallas import tpu as pltpu
from jax.sharding import PartitionSpec as P

LANE_BITS = 7
LANES = 2**LANE_BITS
ROW_BITS = 9
ROWS = 2**ROW_BITS
DIM_BITS = 8
DIM = 2**DIM_BITS

BF16 = jnp.bfloat16
F32 = jnp.float32


def mm(a, b):
    return jnp.dot(a, b, preferred_element_type=F32)


def split(x):
    high = x.astype(BF16)
    low = (x - high.astype(F32)).astype(BF16)
    return high, low


def gate_slots(bits, gate):
    used = [bits[gate, j] - LANE_BITS for j in range(DIM_BITS)]
    free = ROW_BITS * (ROW_BITS - 1) // 2 - sum(used)
    return used + [free]


def plan_slots(plan, start, count, rest, turned=None):
    slots = [plan[start + b] - LANE_BITS for b in range(count)]
    if turned is not None:
        half = count // 2
        slots = [jnp.where(turned == 1, plan[start + (b + half) % count], plan[start + b]) for b in range(count)]
        slots = [slot - LANE_BITS for slot in slots]
    filled = jnp.int32(0)
    for p in range(ROW_BITS):
        rest[filled] = jnp.int32(p)
        taken = functools.reduce(jnp.logical_or, [s == p for s in slots])
        filled = filled + jnp.where(taken, 0, 1).astype(jnp.int32)
    return [rest[k] for k in range(ROW_BITS - count)] + slots


def permutation(source, target, where):
    for place in range(ROW_BITS):
        where[target[place]] = jnp.int32(place)
    lane = lax.broadcasted_iota(jnp.int32, (8, ROWS), 1)
    moved = jnp.zeros((8, ROWS), jnp.int32)
    for place in range(ROW_BITS):
        moved = moved | (((lane >> place) & 1) << where[source[place]])
    row = lax.broadcasted_iota(jnp.int32, (ROWS, ROWS), 0)
    hit = jnp.broadcast_to(moved[:1], (ROWS, ROWS)) == row
    return jnp.where(hit, 1.0, 0.0).astype(BF16)


def stack_gate(real, imag):
    real_high, real_low = split(real)
    imag_high, imag_low = split(imag)
    return jnp.concatenate([real_high, imag_high, real_low, imag_low], axis=0)


def pack_parts(real, imag):
    real_high, real_low = split(real)
    imag_high, imag_low = split(imag)
    return jnp.concatenate([real_high, imag_high, real_low, imag_low], axis=1)


def complex_product(stack, high, low, width):
    half = stack.shape[0] // 2
    quarter = half // 2
    first = mm(stack, high)
    total = first[:half] + first[half:] + mm(stack[:half], low)
    real = total[:quarter, :width] - total[quarter:, width:]
    imag = total[:quarter, width:] + total[quarter:, :width]
    return real, imag


def gate_on_parts(stack, parts, width):
    reals, imags = [], []
    for free in range(2):
        rows = parts[free * DIM : (free + 1) * DIM]
        real, imag = complex_product(stack, rows[:, : 2 * width], rows[:, 2 * width :], width)
        reals.append(real)
        imags.append(imag)
    return jnp.concatenate(reals, axis=0), jnp.concatenate(imags, axis=0)


def first_kernel(narrow_bits, bits, plan, x, gates, out, where, rest):
    natural = list(range(ROW_BITS))
    order_a = gate_slots(bits, 0)
    order_b = gate_slots(bits, 1)
    order_out = plan_slots(plan, 0, narrow_bits, rest)
    parts = pack_parts(x[pl.ds(0, ROWS, stride=2), :], x[pl.ds(1, ROWS, stride=2), :])
    parts = mm(permutation(natural, order_a, where), parts).astype(BF16)
    real, imag = gate_on_parts(stack_gate(gates[0, 0], gates[0, 1]), parts, LANES)
    parts = pack_parts(real, imag)
    parts = mm(permutation(order_a, order_b, where), parts).astype(BF16)
    real, imag = gate_on_parts(stack_gate(gates[1, 0], gates[1, 1]), parts, LANES)
    parts = mm(permutation(order_b, order_out, where), pack_parts(real, imag))
    blocks = out.shape[0]
    shape = (blocks, ROWS // blocks, LANES)
    out[:, 0] = (parts[:, :LANES] + parts[:, 2 * LANES : 3 * LANES]).reshape(shape)
    out[:, 1] = (parts[:, LANES : 2 * LANES] + parts[:, 3 * LANES :]).reshape(shape)


def operator_kernel(section, order_in, order_out, bits, plan, core, gates, out, where, rest):
    order_a = gate_slots(bits, 2 * section)
    order_b = gate_slots(bits, 2 * section + 1)
    columns = order_in(plan, rest, core[0])
    result = order_out(plan, rest, core[0])
    pick = permutation(columns, order_a, where)
    stack = stack_gate(gates[0, 0], gates[0, 1])
    picked = [mm(stack, pick[free * DIM : (free + 1) * DIM]).astype(BF16) for free in range(2)]
    parts = jnp.concatenate(
        [
            jnp.concatenate([p[k * DIM : (k + 1) * DIM] for p in picked], axis=0)
            for k in range(4)
        ],
        axis=1,
    )
    parts = mm(permutation(order_a, order_b, where), parts).astype(BF16)
    real, imag = gate_on_parts(stack_gate(gates[1, 0], gates[1, 1]), parts, ROWS)
    final = permutation(order_b, result, where)
    for k, part in enumerate([*split(real), *split(imag)]):
        place = (k % 2) * 2 + k // 2
        out[place * ROWS : (place + 1) * ROWS, :] = mm(final, part).astype(BF16)


def apply_section(stack, x):
    real = x[:, 0].reshape(ROWS, LANES)
    imag = x[:, 1].reshape(ROWS, LANES)
    real_high, real_low = split(real)
    imag_high, imag_low = split(imag)
    high = jnp.concatenate([real_high, imag_high], axis=1)
    low = jnp.concatenate([real_low, imag_low], axis=1)
    return complex_product(stack, high, low, LANES)


def half_section(stack, x, part):
    rows = stack[...].reshape(4, ROWS, ROWS)[:, part * DIM : (part + 1) * DIM]
    return apply_section(rows.reshape(4 * DIM, ROWS), x[...])


def middle_kernel(stack, x, out):
    blocks = out.shape[0] // 2
    shape = (blocks, DIM // blocks, LANES)
    for part in range(2):
        real, imag = half_section(stack, x, part)
        out[part * blocks : (part + 1) * blocks, 0] = real.reshape(shape)
        out[part * blocks : (part + 1) * blocks, 1] = imag.reshape(shape)


def last_kernel(stack, x, out, held, sems):
    copies = []
    for part in range(2):
        real, imag = half_section(stack, x, part)
        held[part, pl.ds(0, DIM, stride=2), :] = real
        held[part, pl.ds(1, DIM, stride=2), :] = imag
        target = out.at[pl.ds(part * ROWS, ROWS)]
        copies.append(pltpu.make_async_copy(held.at[part], target, sems.at[part]))
        copies[-1].start()
    for copy in copies:
        copy.wait()


SMEM = pl.BlockSpec(memory_space=pltpu.SMEM)
VMEM = pl.BlockSpec(memory_space=pltpu.VMEM)
ANY = pl.BlockSpec(memory_space=pl.ANY)
SCALARS = [pltpu.SMEM((ROW_BITS,), jnp.int32), pltpu.SMEM((ROW_BITS + 1,), jnp.int32)]
UNIT = 2 * DIM**3


def gates_spec(section):
    return pl.BlockSpec((2, 2, DIM, DIM), lambda i: (section, 0, 0, 0))


def cost(units, moved):
    return pl.CostEstimate(flops=units * UNIT, bytes_accessed=moved, transcendentals=0)


def first_section(x, gates, bits, plan, narrow_bits):
    blocks = 2**narrow_bits
    shape = (blocks, 2, ROWS // blocks, LANES)
    return pl.pallas_call(
        functools.partial(first_kernel, narrow_bits),
        grid=(1,),
        out_shape=vmem_shape(shape, F32),
        in_specs=[SMEM, SMEM, VMEM, gates_spec(0)],
        out_specs=VMEM,
        scratch_shapes=SCALARS,
        cost_estimate=cost(48, 2 * 2**20),
        name="first_section",
    )(bits, plan, x, gates)


def section_operator(section, gates, bits, plan, core, order_in, order_out):
    return pl.pallas_call(
        functools.partial(operator_kernel, section, order_in, order_out),
        grid=(1,),
        out_shape=vmem_shape((4 * ROWS, ROWS), BF16),
        in_specs=[SMEM, SMEM, SMEM, gates_spec(section)],
        out_specs=VMEM,
        scratch_shapes=SCALARS,
        cost_estimate=cost(128, 3 * 2**20),
        compiler_params=pltpu.CompilerParams(vmem_limit_bytes=40 * 2**20),
        name="section_operator",
    )(bits, plan, core, gates)


def vmem_shape(shape, dtype):
    return pltpu.VMEM(shape, dtype)


def in_vmem(x):
    return pltpu.with_memory_space_constraint(x, pltpu.VMEM)


def run_section(kernel, stack, x, out_shape, name, out_specs=None, scratch_shapes=()):
    return pl.pallas_call(
        kernel,
        out_shape=out_shape,
        in_specs=[VMEM, VMEM],
        out_specs=VMEM if out_specs is None else out_specs,
        scratch_shapes=scratch_shapes,
        cost_estimate=cost(24, 3 * 2**20),
        name=name,
    )(in_vmem(stack), in_vmem(x))


def exchange_narrow(blocks):
    flat = blocks.reshape(blocks.shape[0], -1, LANES)
    flat = lax.all_to_all(flat, "narrow", split_axis=0, concat_axis=0, tiled=True)
    return flat.reshape(blocks.shape)


def wide_groups(wide, narrow, high_on_even):
    side = 2 ** ((wide.bit_length() - 1) // 2)
    other = wide // side
    groups = []
    for n in range(narrow):
        if (n % 2 == 0) == high_on_even:
            groups += [[(j * side + k) * narrow + n for j in range(other)] for k in range(side)]
        else:
            groups += [[(k * side + j) * narrow + n for j in range(side)] for k in range(other)]
    return groups


def exchange_wide(blocks, wide, narrow):
    side = 2 ** ((wide.bit_length() - 1) // 2)
    square = blocks.reshape(side, side, -1, LANES)
    for turn in range(2):
        if turn:
            square = square.transpose(1, 0, 2, 3)
        square = lax.all_to_all(
            square,
            ("wide", "narrow"),
            split_axis=0,
            concat_axis=0,
            tiled=True,
            axis_index_groups=wide_groups(wide, narrow, turn == 0),
        )
    return square.reshape(blocks.shape)


def shards(state, gates, gate_bits, slot_plan):
    narrow = lax.axis_size("narrow")
    wide = lax.axis_size("wide")
    narrow_bits = narrow.bit_length() - 1
    wide_bits = wide.bit_length() - 1
    core = (lax.axis_index("narrow") % 2).astype(jnp.int32).reshape(1)
    x = state.reshape(2, ROWS, LANES).transpose(1, 0, 2).reshape(2 * ROWS, LANES)

    def narrow_order(plan, rest, core):
        return plan_slots(plan, 0, narrow_bits, rest)

    def wide_order(plan, rest, core):
        return plan_slots(plan, narrow_bits, wide_bits, rest, core)

    def turned_order(plan, rest, core):
        return plan_slots(plan, narrow_bits, wide_bits, rest, 1 - core)

    def natural(plan, rest, core):
        return list(range(ROW_BITS))

    blocks = first_section(x, gates, gate_bits, slot_plan, narrow_bits)
    second = section_operator(1, gates, gate_bits, slot_plan, core, narrow_order, wide_order)
    third = section_operator(2, gates, gate_bits, slot_plan, core, turned_order, natural)
    second, third = lax.optimization_barrier((second, third))
    blocks = exchange_narrow(blocks)
    shape = vmem_shape((wide, 2, ROWS // wide, LANES), F32)
    blocks = run_section(middle_kernel, second, blocks, shape, "middle_section")
    blocks = exchange_wide(blocks, wide, narrow)
    shape = jax.ShapeDtypeStruct((2 * ROWS, LANES), F32)
    held = [pltpu.VMEM((2, ROWS, LANES), F32), pltpu.SemaphoreType.DMA((2,))]
    x = run_section(last_kernel, third, blocks, shape, "last_section", ANY, held)
    return x.reshape(ROWS, 2, LANES).transpose(1, 0, 2).reshape(2, ROWS * LANES)


def solution(mesh):
    return jax.shard_map(
        shards,
        mesh=mesh,
        in_specs=(P(None, ("wide", "narrow")), P(), P(), P()),
        out_specs=P(None, ("wide", "narrow")),
        check_vma=False,
    )
```
